32 devices in a mesh: grp: 2 (over x), seq: 8 (over z, y), col: 2 (over core).
Axes of the slice: x: 2, y: 2, z: 4, core: 2. Of those that a mesh axis runs over, the one named last changes fastest.
Arguments:
- signal: bfloat16 [8192, 1408], P(('grp', 'seq'), 'col'), parts along dimension 0, may hold values from -6 to 6
- conv_weight: bfloat16 [5, 1408, 1408], P(None, None, 'col'), may hold values from -0.15625 to 0.15625
- conv_gain: float32 [1408], replicated, may hold values from 0.1 to 1.9
- embed_weight: bfloat16 [1408, 1536], P('col', 'seq'), may hold values from -0.15625 to 0.15625
- attn_gain: float32 [1536], replicated, may hold values from 0.1 to 1.9
- query_weight: bfloat16 [1536, 1024], P('seq'), may hold values from -4 to 4
- keyvalue_weight: bfloat16 [1536, 320], P('seq'), may hold values from -4 to 4
- output_weight: bfloat16 [1536, 1536], P(None, 'seq'), may hold values from -0.15625 to 0.15625
- rowcol_weight: bfloat16 [1536, 256], replicated, may hold values from -0.15625 to 0.15625
- pair_weight: bfloat16 [128, 128], replicated, may hold values from -0.5 to 0.5
Outputs:
- tokens: bfloat16 [2048, 1536], P(('grp', 'seq', 'col')), parts along dimension 0
- pair_out: bfloat16 [128, 64, 128], P(('grp', 'seq'), 'col'), parts along dimension 0
The draws below stay inside these ranges and needn't reach their ends.
There are 2 independent parts, one for each index of `grp`. The reference program is written for one: setup_inputs(seed, part) draws one part's arguments, and reference() takes and returns one part's arrays. A program takes and returns all parts, laid end to end along the dimension named above; an argument that names none is the same for every part. Nothing has to cross between parts.
All inputs are finite; a program needn't handle non-finite values.
Results may differ from the reference program's by a relative error of at most 0.015.
Values may be sent and summed in bfloat16 or wider, within the bound.
A program may use at most 128 MiB of HBM per device.

```python
import math
import jax
import jax.numpy as jnp
from jax import lax

C = 1408
D = 1536
H = 8
DK = 128
DV = 192
F = 128
TAPS = 5
POOL = 4
PAIR_POOL = 16
L = 4096


def key_matrix(key):
    return jax.random.truncated_normal(jax.random.fold_in(key, 11), -6.0, 6.0, (D, DK), jnp.float32) / math.sqrt(D)


def draw_keyvalue_weight(key, part):
    keys = key_matrix(key)
    values = jax.random.truncated_normal(jax.random.fold_in(key, 12), -6.0, 6.0, (D, DV), jnp.float32) / math.sqrt(D)
    return jnp.clip(jnp.concatenate([keys, values], axis=1), -4.0, 4.0).astype(jnp.bfloat16)


def draw_query_weight(key, part):
    noise = jax.random.truncated_normal(jax.random.fold_in(key, 13), -6.0, 6.0, (D, H * DK), jnp.float32) * (2.0 / math.sqrt(D))
    result = noise
    return jnp.clip(result, -4.0, 4.0).astype(jnp.bfloat16)


def block_scale(stream_key, shape, split, least, top_value):
    loudness = 1.0
    for dim, shards_of in split:
        heights = jax.random.uniform(jax.random.fold_in(jax.random.fold_in(stream_key, 6), dim), (shards_of,), jnp.float32, least / len(split), top_value / len(split))
        loudness = loudness * jnp.repeat(jnp.exp(heights), shape[dim] // shards_of).reshape((-1,) + (1,) * (len(shape) - 1 - dim))
    return loudness


def scatter_about(key, shape, scale, most, cuts=(), kind=jnp.bfloat16):
    gain = block_scale(key, shape, cuts, -0.22, 0.18) if cuts else 1.0
    values = jax.random.normal(key, shape, jnp.float32) * scale * gain
    return jnp.minimum(jnp.maximum(values, -most), most).astype(kind)


def setup_inputs(seed: int = 0, part: int = 0) -> dict:
    arg_keys = jax.random.split(jax.random.key(seed), 11)
    own_keys = jax.random.split(jax.random.fold_in(arg_keys[10], part), 11)
    return {
        "signal": scatter_about(own_keys[0], (L, C), 1.0, 6.0, ((0, 8), (1, 2))),
        "conv_weight": scatter_about(arg_keys[1], (TAPS, C, C), C ** -0.5, 0.15625, ((2, 2),)),
        "conv_gain": jnp.clip(1.0 + 0.18 * jax.random.normal(arg_keys[2], (C,), jnp.float32), 0.1, 1.9),
        "embed_weight": scatter_about(arg_keys[3], (C, D), C ** -0.5, 0.15625, ((0, 2), (1, 8))),
        "attn_gain": jnp.clip(1.0 + 0.18 * jax.random.normal(arg_keys[4], (D,), jnp.float32), 0.1, 1.9),
        "query_weight": draw_query_weight(jax.random.fold_in(arg_keys[10], 71), part),
        "keyvalue_weight": draw_keyvalue_weight(jax.random.fold_in(arg_keys[10], 71), part),
        "output_weight": scatter_about(arg_keys[7], (H * DV, D), (H * DV) ** -0.5, 0.15625, ((1, 8),)),
        "rowcol_weight": scatter_about(arg_keys[8], (D, 2 * F), D ** -0.5, 0.15625),
        "pair_weight": scatter_about(arg_keys[9], (F, F), F ** -0.5, 0.5),
    }


def rms_scale(values, gain_vector):
    return values * lax.rsqrt(lax.optimization_barrier(jnp.mean(values * values, axis=-1, keepdims=True)) + 1e-06) * gain_vector

def reference(signal, conv_weight, conv_gain, embed_weight, attn_gain, query_weight, keyvalue_weight, output_weight, rowcol_weight, pair_weight):
    length = signal.shape[0]
    features_in = signal.astype(jnp.float32)
    activated = jax.nn.gelu(rms_scale(features_in, conv_gain.astype(jnp.float32)), approximate=True).astype(jnp.bfloat16)
    half_width = TAPS // 2
    padded = jnp.pad(activated, ((half_width, half_width), (0, 0)))
    summed = features_in
    for tap_index in range(TAPS):
        summed = summed + jnp.dot(padded[tap_index:tap_index + length], conv_weight[tap_index], preferred_element_type=jnp.float32)
    pooled = lax.optimization_barrier(jnp.mean(summed.reshape(length // POOL, POOL, -1), axis=1)).astype(jnp.bfloat16)
    embedded = jnp.dot(pooled, embed_weight, preferred_element_type=jnp.float32).astype(jnp.bfloat16)
    normed = rms_scale(embedded.astype(jnp.float32), attn_gain.astype(jnp.float32)).astype(jnp.bfloat16)
    queries = (jnp.dot(normed, query_weight, preferred_element_type=jnp.float32) * DK ** (-0.5)).astype(jnp.bfloat16)
    keyvalue = jnp.dot(normed, keyvalue_weight, preferred_element_type=jnp.float32).astype(jnp.bfloat16)
    keys = keyvalue[:, :DK]
    values = keyvalue[:, DK:]
    token_count = queries.shape[0]
    per_head = jnp.transpose(queries.reshape(token_count, H, DK), (1, 0, 2))

    def one_head(head_queries):
        scores = lax.dot_general(head_queries, keys, (((1,), (1,)), ((), ())), preferred_element_type=jnp.float32)
        peak = lax.optimization_barrier(jnp.max(scores, axis=1, keepdims=True))
        weights = jnp.exp(scores - peak)
        total = lax.optimization_barrier(jnp.sum(weights, axis=1, keepdims=True))
        mixed = jnp.dot(weights.astype(jnp.bfloat16), values, preferred_element_type=jnp.float32) / total
        return mixed.astype(jnp.bfloat16)
    attended = lax.map(one_head, per_head)
    attended = jnp.transpose(attended, (1, 0, 2)).reshape(token_count, H * DV)
    attention_out = jnp.dot(attended, output_weight, preferred_element_type=jnp.float32)
    tokens = (embedded.astype(jnp.float32) + attention_out).astype(jnp.bfloat16)
    pair_pool = lax.optimization_barrier(jnp.mean(tokens.astype(jnp.float32).reshape(token_count // PAIR_POOL, PAIR_POOL, -1), axis=1)).astype(jnp.bfloat16)
    projected = jnp.dot(pair_pool, rowcol_weight, preferred_element_type=jnp.float32).astype(jnp.bfloat16)
    row_part = projected[:, :F].astype(jnp.float32)
    column_part = projected[:, F:].astype(jnp.float32)
    hidden = jax.nn.gelu(row_part[:, None, :] + column_part[None, :, :], approximate=True).astype(jnp.bfloat16)
    pair_rows = hidden.shape[0]
    pair_out = jnp.dot(hidden.reshape(-1, F), pair_weight, preferred_element_type=jnp.float32).astype(jnp.bfloat16)
    return (tokens, pair_out.reshape(pair_rows, pair_rows, F))
```

```python
import functools

import jax
import jax.numpy as jnp
from jax import lax
from jax.experimental import pallas as pl
from jax.experimental.pallas import tpu as pltpu
from jax.sharding import PartitionSpec as P

DK = 128
DV = 192
POOL = 4
PAIR_POOL = 16


def with_halo(array, sides, width):
    for axis, dim in sides:
        size, length = (lax.axis_size(axis), array.shape[dim])
        up = [(i, (i + 1) % size) for i in range(size - 1)]
        down = [(j, i) for i, j in up]
        last = lax.slice_in_dim(array, length - width, length, axis=dim)
        first = lax.slice_in_dim(array, 0, width, axis=dim)
        before = lax.ppermute(last, axis, up)
        after = lax.ppermute(first, axis, down)
        array = jnp.concatenate([before, array, after], axis=dim)
    return array


def rms_scale(values, gain_vector):
    return (
        values * lax.rsqrt(jnp.mean(values * values, axis=-1, keepdims=True) + 1e-06) * gain_vector
    )


def attention_parts(queries, head_count):
    query_rows = queries.reshape(queries.shape[0] * head_count, DK)

    def absorb(running, pieces, first_row):
        running_max, running_sum, accumulated = running
        key_piece, value_piece = pieces
        scores = lax.dot_general(
            query_rows, key_piece, (((1,), (1,)), ((), ())), preferred_element_type=jnp.float32
        )
        newest_max = jnp.maximum(running_max, jnp.max(scores, axis=1))
        weights = jnp.exp(scores - newest_max[:, None])
        running_sum = jnp.sum(weights, axis=1)
        accumulated = jnp.dot(
            weights.astype(jnp.bfloat16), value_piece, preferred_element_type=jnp.float32
        )
        return (newest_max, running_sum, accumulated)

    row_count = query_rows.shape[0]
    initial = (
        jnp.full((row_count,), -1e30, jnp.float32),
        jnp.zeros((row_count,), jnp.float32),
        jnp.zeros((row_count, DV), jnp.float32),
    )
    return (absorb, initial)


def finish_attention(result, token_count):
    running_max, running_sum, accumulated = result
    return (accumulated / running_sum[:, None]).astype(jnp.bfloat16).reshape(token_count, -1)


def on_device(
    signal,
    conv_weight,
    conv_gain,
    embed_weight,
    attn_gain,
    query_weight,
    keyvalue_weight,
    output_weight,
    rowcol_weight,
    pair_weight,
):
    positions = signal.shape[0]
    tap_count = conv_weight.shape[0]
    halo_width = tap_count // 2
    padded = with_halo(signal, (("seq", 0),), halo_width)
    widened = lax.all_gather(padded, "col", axis=1, tiled=True)
    activated = jax.nn.gelu(
        rms_scale(widened.astype(jnp.float32), conv_gain), approximate=True
    ).astype(jnp.bfloat16)
    summed = signal.astype(jnp.float32)
    for tap_index in range(tap_count):
        summed = summed + jnp.dot(
            activated[tap_index : tap_index + positions],
            conv_weight[tap_index],
            preferred_element_type=jnp.float32,
        )
    pooled = jnp.mean(summed.reshape(positions // POOL, POOL, -1), axis=1).astype(jnp.bfloat16)
    embed_full = lax.all_gather(embed_weight, "seq", axis=1, tiled=True)
    col_count = lax.axis_size("col")
    embedded = lax.psum_scatter(
        jnp.dot(pooled, embed_full, preferred_element_type=jnp.float32).astype(jnp.bfloat16),
        "col",
        scatter_dimension=0,
        tiled=True,
    )
    normed = rms_scale(embedded.astype(jnp.float32), attn_gain).astype(jnp.bfloat16)
    head_count = query_weight.shape[1] // DK
    scaling = DK ** (-0.5)
    col_index = lax.axis_index("col")
    local_heads = head_count // col_count
    group_tokens = lax.all_gather(normed, "col", axis=0, tiled=True)
    group_count = group_tokens.shape[0]
    query_half = lax.dynamic_slice_in_dim(
        query_weight, col_index * local_heads * DK, local_heads * DK, 1
    )
    query_sum = jnp.dot(
        group_tokens,
        lax.all_gather(query_half, "seq", axis=0, tiled=True),
        preferred_element_type=jnp.float32,
    )
    keyvalue_sum = jnp.dot(
        group_tokens,
        lax.all_gather(keyvalue_weight, "seq", axis=0, tiled=True),
        preferred_element_type=jnp.float32,
    )
    queries = (query_sum * scaling).astype(jnp.bfloat16)
    keyvalue = keyvalue_sum.astype(jnp.bfloat16)
    absorb, initial = attention_parts(queries, local_heads)
    result = absorb(
        initial,
        (
            lax.all_gather(keyvalue[:, :DK], "seq", axis=0, tiled=True),
            lax.all_gather(keyvalue[:, DK:], "seq", axis=0, tiled=True),
        ),
        jnp.int32(0),
    )
    attended = finish_attention(result, group_count)
    output_half = lax.dynamic_slice_in_dim(
        output_weight, col_index * local_heads * DV, local_heads * DV, 0
    )
    partial_out = jnp.dot(
        attended,
        lax.all_gather(output_half, "seq", axis=1, tiled=True),
        preferred_element_type=jnp.float32,
    )
    attention_out = lax.psum_scatter(
        partial_out.astype(jnp.bfloat16), "col", scatter_dimension=0, tiled=True
    ).astype(jnp.float32)
    tokens = (embedded.astype(jnp.float32) + attention_out).astype(jnp.bfloat16)
    pair_pool = jnp.mean(
        tokens.astype(jnp.float32).reshape(-1, PAIR_POOL, tokens.shape[1]), axis=1
    ).astype(jnp.bfloat16)
    projected = jnp.dot(pair_pool, rowcol_weight, preferred_element_type=jnp.float32).astype(
        jnp.bfloat16
    )
    features = pair_weight.shape[0]
    row_block = lax.all_gather(projected, "col", axis=0, tiled=True)
    column_all = lax.all_gather(row_block[:, features:], "seq", axis=0, tiled=True)
    row_part = row_block[:, :features]
    column_span = column_all.shape[0] // col_count
    column_part = lax.dynamic_slice_in_dim(
        column_all, lax.axis_index("col") * column_span, column_span, 0
    )
    hidden = jax.nn.gelu(
        row_part.astype(jnp.float32)[:, None, :] + column_part.astype(jnp.float32)[None, :, :],
        approximate=True,
    ).astype(jnp.bfloat16)
    pair_out = jnp.dot(
        hidden.reshape(-1, features), pair_weight, preferred_element_type=jnp.float32
    ).astype(jnp.bfloat16)
    return (tokens, pair_out.reshape(row_part.shape[0], column_span, features))


EDGE = 16
LEAD = 8
Y = 2


def fused_kernel(
    taps,
    heads,
    signal,
    conv_w,
    conv_gain,
    embed_w,
    attn_gain,
    query_w,
    kv_w,
    out_w,
    rowcol,
    pair_w,
    tokens_out,
    pair_out,
    sig,
    act,
    halo,
    conv_buf,
    e_buf,
    q_buf,
    k_buf,
    o_buf,
    part,
    other,
    emb,
    normed,
    kv_all,
    att,
    cols,
    hid,
    loc_sem,
    sig_sem,
    w_sem,
    p_sem,
    kv_sem,
    kp_sem,
    ex_sem,
    col_sem,
):
    f32, bf16 = jnp.float32, jnp.bfloat16
    n = lax.axis_size("seq")
    nz = n // Y
    s = lax.axis_index("seq")
    c = lax.axis_index("col")
    x = lax.axis_index("grp")
    z, y = s // Y, s % Y
    half = sig.shape[2]
    positions = sig.shape[1]
    count = positions // POOL
    width = e_buf.shape[2]
    halo_width = taps // 2
    started = []

    def remote(src, dst, sems, index, to):
        copy = pltpu.make_async_remote_copy(
            src_ref=src,
            dst_ref=dst,
            send_sem=sems.at[(0,) + index],
            recv_sem=sems.at[(1,) + index],
            device_id=to,
            device_id_type=pl.DeviceIdType.MESH,
        )
        copy.start()
        started.append(copy)
        return copy

    def seq_of(z_index, y_index):
        return z_index * Y + y_index

    def z_from(dz):
        return (z + nz - dz) % nz

    def z_to(dz):
        return (z + dz) % nz

    partner = {"col": 1 - c}
    y_peer = {"seq": seq_of(z, 1 - y)}
    x_peer = {"grp": 1 - x}

    local = [pltpu.make_async_copy(signal, sig.at[0], loc_sem.at[0])]
    local[0].start()
    k_rows = kv_w.shape[0] // 2
    q_cols = query_w.shape[1] // 2
    o_rows = out_w.shape[0] // 2
    kv_own = kv_w.at[pl.ds(pl.multiple_of(c * k_rows, 16), k_rows)]
    q_own = query_w.at[:, pl.ds(pl.multiple_of(c * q_cols, 128), q_cols)]
    o_own = out_w.at[pl.ds(pl.multiple_of(c * o_rows, 16), o_rows)]

    def e_at(owner):
        return e_buf.at[owner]

    def q_at(owner):
        return q_buf.at[owner]

    def k_at(owner, core=None):
        core = c if core is None else core
        return k_buf.at[owner, pl.ds(pl.multiple_of(core * k_rows, 16), k_rows)]

    def o_at(owner):
        return o_buf.at[owner]

    pieces = [(embed_w, e_at), (kv_own, k_at), (q_own, q_at), (o_own, o_at)]
    E, KV, Q, O = range(4)
    for t in range(taps):
        local.append(pltpu.make_async_copy(conv_w.at[t], conv_buf.at[t], loc_sem.at[1 + t]))
    for w, (own, at) in enumerate(pieces):
        local.append(pltpu.make_async_copy(own, at(s), loc_sem.at[1 + taps + w]))
    for copy in local[1:]:
        copy.start()

    barrier = pltpu.get_barrier_semaphore()
    for d in range(n):
        for e in range(2):
            if d or e:
                pl.semaphore_signal(
                    barrier,
                    inc=1,
                    device_id={"seq": (s + d) % n, "col": (c + e) % 2},
                    device_id_type=pl.DeviceIdType.MESH,
                )
    pl.semaphore_signal(barrier, inc=1, device_id=x_peer, device_id_type=pl.DeviceIdType.MESH)
    pl.semaphore_wait(barrier, 2 * n)

    signal_copies = [remote(signal, sig.at[1], sig_sem, (0,), partner)]
    last = signal.at[pl.ds(positions - EDGE, EDGE)]
    first = signal.at[pl.ds(0, EDGE)]
    for e in range(2):
        core = (c + e) % 2
        up = {"seq": (s + 1) % n, "col": core}
        down = {"seq": (s + n - 1) % n, "col": core}
        signal_copies.append(remote(last, halo.at[e, 0], sig_sem, (1 + 2 * e,), up))
        signal_copies.append(remote(first, halo.at[e, 1], sig_sem, (2 + 2 * e,), down))

    def rows_half(ref, h):
        rows = ref.shape[0] // 2
        return ref.at[pl.ds(pl.multiple_of(h * rows, 16), rows)]

    copies = {}

    def send(w, key, slot, src, dst, to):
        copies[w, key] = remote(src, dst, w_sem, (w, slot), to)

    def along_z(w):
        own, at = pieces[w]
        for dz in range(1, nz):
            to = {"seq": seq_of(z_to(dz), y)}
            send(w, ("z", dz), dz, rows_half(own, x), rows_half(at(s), x), to)

    def own_y(w):
        own, at = pieces[w]
        send(w, ("y", 0), 0, own, at(s), y_peer)

    def stage2(w):
        _, at = pieces[w]
        for dz in range(1, nz):
            copies[w, ("z", dz)].wait_recv()
            ref = rows_half(at(seq_of(z_from(dz), y)), x)
            send(w, ("y", dz), nz + dz, ref, ref, y_peer)
            send(w, ("x", dz), 2 * nz + dz, ref, ref, x_peer)

    def stage3(w):
        _, at = pieces[w]
        for dz in range(1, nz):
            copies[w, ("y", dz)].wait_recv()
            ref = rows_half(at(seq_of(z_from(dz), 1 - y)), x)
            send(w, ("xy", dz), 3 * nz + dz, ref, ref, x_peer)

    def owners():
        order = [(0, True), (0, False)]
        for dz in range(1, nz):
            order += [(dz, True), (dz, False)]
        return order

    def owner_of(dz, same):
        return seq_of(z_from(dz), y if same else 1 - y)

    def arrived(w, dz, same):
        if dz == 0:
            if same:
                local[1 + taps + w].wait()
            else:
                copies[w, ("y", 0)].wait_recv()
        else:
            copies[w, ("x" if same else "xy", dz)].wait_recv()

    along_z(E)
    own_y(E)
    along_z(KV)
    along_z(Q)
    along_z(O)

    for copy in signal_copies:
        copy.wait_recv()
    local[0].wait()
    inside = [s > 0, s < n - 1]

    def squares(v):
        return jnp.sum(v * v, axis=1, keepdims=True)

    channels = 2 * half
    gains = [conv_gain[pl.ds(c, 1), :], conv_gain[pl.ds(1 - c, 1), :]]

    def activate(v, scale, gain):
        return jax.nn.gelu(v * scale * gain, approximate=True)

    block = 64
    lanes = act.shape[3]
    tiles = [(q, min(lanes, half - q * lanes)) for q in range(act.shape[1])]

    def put_rows(h, rows, v):
        for q, size in tiles:
            act[h, q, rows, :size] = v[:, q * lanes : q * lanes + size]

    def pooled_rows(h, begin):
        out = []
        for q, size in tiles:
            v = act[h, q, pl.ds(begin, count, stride=POOL), :]
            for j in range(1, POOL):
                v = v + act[h, q, pl.ds(begin + j, count, stride=POOL), :]
            out.append((v * (1.0 / POOL))[:, :size])
        return jnp.concatenate(out, axis=1)

    @pl.loop(0, positions // block)
    def _(i):
        rows = pl.ds(pl.multiple_of(i * block, block), block)
        put = pl.ds(pl.multiple_of(LEAD + i * block, 8), block)
        a, b = sig[0, rows, :].astype(f32), sig[1, rows, :].astype(f32)
        scale = lax.rsqrt((squares(a) + squares(b)) * (1.0 / channels) + 1e-06)
        put_rows(0, put, activate(a, scale, gains[0]))
        put_rows(1, put, activate(b, scale, gains[1]))

    for side in range(2):
        a, b = halo[0, side].astype(f32), halo[1, side].astype(f32)
        scale = lax.rsqrt((squares(a) + squares(b)) * (1.0 / channels) + 1e-06)
        for h, v in enumerate((a, b)):
            v = jnp.where(inside[side], activate(v, scale, gains[h]), 0.0)
            if side == 0:
                put_rows(h, pl.ds(0, LEAD), v[EDGE - LEAD :])
            else:
                put_rows(h, pl.ds(LEAD + positions, LEAD), v[:LEAD])

    stage2(E)

    total = jnp.zeros((count, half), f32)
    for t in range(taps):
        local[1 + t].wait()
        for h in range(2):
            window = pooled_rows(h, LEAD + t - halo_width).astype(bf16)
            core = c if h == 0 else 1 - c
            rows = pl.ds(pl.multiple_of(core * half, 16), half)
            total = total + jnp.dot(window, conv_buf[t, rows, :], preferred_element_type=f32)

    @pl.loop(0, positions // block)
    def _(i):
        rows = pl.ds(pl.multiple_of(i * block, block), block)
        put = pl.ds(pl.multiple_of(LEAD + i * block, 8), block)
        put_rows(0, put, sig[0, rows, :].astype(f32))

    pooled = (total + pooled_rows(0, LEAD)).astype(bf16)

    stage3(E)
    own_y(KV)
    own_y(Q)

    swaps = []
    for k, (dz, same) in enumerate(owners()):
        owner = owner_of(dz, same)
        arrived(E, dz, same)
        part[0, owner] = jnp.dot(pooled, e_buf[owner], preferred_element_type=f32).astype(bf16)
        swaps.append(remote(part.at[0, owner], other.at[0, owner], ex_sem, (0, k), partner))
    stage2(KV)
    stage2(Q)
    for copy in swaps:
        copy.wait_recv()
    square = jnp.zeros((count, 1), f32)
    for b in range(n):
        v = (part[0, b].astype(f32) + other[0, b].astype(f32)).astype(bf16)
        emb[b] = v
        square = square + squares(v.astype(f32))
    scale = lax.rsqrt(square * (1.0 / (n * width)) + 1e-06)
    for b in range(n):
        normed[b] = (emb[b].astype(f32) * scale * attn_gain[pl.ds(b, 1), :]).astype(bf16)

    stage3(KV)
    stage3(Q)
    own_y(O)

    passed = []
    for k, (dz, same) in enumerate(owners()):
        arrived(KV, dz, same)
        ref = k_at(owner_of(dz, same))
        passed.append(remote(ref, ref, p_sem, (k,), partner))
    for copy in passed:
        copy.wait_recv()
    own_tokens = pl.ds(pl.multiple_of(c * (count // 2), 16), count // 2)
    kv = jnp.zeros((count // 2, k_buf.shape[2]), f32)
    for b in range(n):
        kv = kv + jnp.dot(normed[b, own_tokens, :], k_buf[b], preferred_element_type=f32)

    def kv_at(owner):
        return kv_all.at[owner, own_tokens]

    kv_all[s, own_tokens, :] = kv.astype(bf16)
    mine = kv_at(s)
    kv_copies = {}
    for dz in range(1, nz):
        to = {"seq": seq_of(z_to(dz), y)}
        kv_copies["z", dz] = remote(mine, mine, kv_sem, (dz,), to)
    kv_copies["y", 0] = remote(mine, mine, kv_sem, (0,), y_peer)
    across = [remote(mine, mine, kp_sem, (0,), partner)]

    queries = jnp.zeros((count, q_cols), f32)
    for dz, same in owners():
        arrived(Q, dz, same)
    for b in range(n):
        queries = queries + jnp.dot(normed[b], q_buf[b], preferred_element_type=f32)
    queries = (queries * (DK**-0.5)).astype(bf16)

    for dz in range(1, nz):
        kv_copies["z", dz].wait_recv()
        ref = kv_at(seq_of(z_from(dz), y))
        kv_copies["y", dz] = remote(ref, ref, kv_sem, (nz + dz,), y_peer)
        across.append(remote(ref, ref, kp_sem, (dz,), partner))
    stage2(O)
    for dz in range(nz):
        kv_copies["y", dz].wait_recv()
        ref = kv_at(seq_of(z_from(dz), 1 - y))
        across.append(remote(ref, ref, kp_sem, (nz + dz,), partner))
    for copy in across:
        copy.wait_recv()

    everything = kv_all[...].reshape(n * count, kv_all.shape[2])
    keys, values = everything[:, :DK], everything[:, DK:]
    for h in range(heads):
        scores = lax.dot_general(
            queries[:, h * DK : (h + 1) * DK],
            keys,
            (((1,), (1,)), ((), ())),
            preferred_element_type=f32,
        )
        weights = jnp.exp(scores - jnp.max(scores, axis=1, keepdims=True))
        norm = jnp.sum(weights, axis=1, keepdims=True)
        mixed = jnp.dot(weights.astype(bf16), values, preferred_element_type=f32)
        att[h] = (mixed / norm).astype(bf16)

    stage3(O)
    swaps = []
    for k, (dz, same) in enumerate(owners()):
        owner = owner_of(dz, same)
        arrived(O, dz, same)
        acc = jnp.zeros((count, width), f32)
        for h in range(heads):
            acc = acc + jnp.dot(
                att[h], o_buf[owner, h * DV : (h + 1) * DV, :], preferred_element_type=f32
            )
        part[1, owner] = acc.astype(bf16)
        swaps.append(remote(part.at[1, owner], other.at[1, owner], ex_sem, (1, k), partner))
    for copy in swaps:
        copy.wait_recv()

    rows_n = count // PAIR_POOL
    row_of = lax.broadcasted_iota(jnp.int32, (rows_n, count), 0)
    token_of = lax.broadcasted_iota(jnp.int32, (rows_n, count), 1) // PAIR_POOL
    pool = jnp.where(row_of == token_of, 1.0 / PAIR_POOL, 0.0).astype(bf16)
    features = pair_w.shape[0]
    projected = jnp.zeros((rows_n, 2 * features), f32)
    for b in range(n):
        v = emb[b].astype(f32) + (part[1, b].astype(f32) + other[1, b].astype(f32))
        emb[b] = v.astype(bf16)
        pair_pool = jnp.dot(pool, emb[b], preferred_element_type=f32).astype(bf16)
        projected = projected + jnp.dot(pair_pool, rowcol[b], preferred_element_type=f32)
    projected = projected.astype(bf16).astype(f32)
    cols[s] = projected[:, features:]
    col_copies = []
    for d in range(1, n):
        to = {"seq": (s + d) % n}
        col_copies.append(remote(cols.at[s], cols.at[s], col_sem, (d,), to))
    for b in range(n):
        tokens_out[b] = emb[b, own_tokens, :]
    for copy in col_copies:
        copy.wait_recv()
    row_part = projected[:, None, :features]
    for j in range(n // 2):
        column = cols[c * (n // 2) + j]
        hid[:, pl.ds(j * rows_n, rows_n), :] = jax.nn.gelu(
            row_part + column[None, :, :], approximate=True
        )
    hidden = hid[...].reshape(rows_n * (n // 2) * rows_n, features).astype(bf16)
    result = jnp.dot(hidden, pair_w[...], preferred_element_type=f32)
    pair_out[...] = result.reshape(pair_out.shape).astype(bf16)
    for copy in started:
        copy.wait_send()


def on_device_fused(
    signal,
    conv_weight,
    conv_gain,
    embed_weight,
    attn_gain,
    query_weight,
    keyvalue_weight,
    output_weight,
    rowcol_weight,
    pair_weight,
):
    bf16, f32 = jnp.bfloat16, jnp.float32
    n = lax.axis_size("seq")
    nz = n // Y
    positions, half = signal.shape
    taps, channels, _ = conv_weight.shape
    count = positions // POOL
    width = embed_weight.shape[1]
    q_cols = query_weight.shape[1] // 2
    heads = q_cols // DK
    kv_cols = keyvalue_weight.shape[1]
    rows_n = count // PAIR_POOL
    features = pair_weight.shape[0]
    any_spec = pl.BlockSpec(memory_space=pl.ANY)
    vmem = pl.BlockSpec(memory_space=pltpu.VMEM)
    dma = pltpu.SemaphoreType.DMA
    tokens, pair = pl.pallas_call(
        functools.partial(fused_kernel, taps, heads),
        out_shape=(
            jax.ShapeDtypeStruct((n, count // 2, width), bf16),
            jax.ShapeDtypeStruct((rows_n, rows_n * n // 2, features), bf16),
        ),
        in_specs=[any_spec, any_spec, vmem, any_spec, vmem]
        + [any_spec, any_spec, any_spec, vmem, vmem],
        out_specs=(vmem, vmem),
        scratch_shapes=[
            pltpu.VMEM((2, positions, half), bf16),
            pltpu.VMEM((2, pl.cdiv(half, 128), positions + 2 * LEAD, 128), f32),
            pltpu.VMEM((2, 2, EDGE, half), bf16),
            pltpu.VMEM((taps, channels, half), bf16),
            pltpu.VMEM((n, half, width), bf16),
            pltpu.VMEM((n, width, q_cols), bf16),
            pltpu.VMEM((n, width, kv_cols), bf16),
            pltpu.VMEM((n, heads * DV, width), bf16),
            pltpu.VMEM((2, n, count, width), bf16),
            pltpu.VMEM((2, n, count, width), bf16),
            pltpu.VMEM((n, count, width), bf16),
            pltpu.VMEM((n, count, width), bf16),
            pltpu.VMEM((n, count, kv_cols), bf16),
            pltpu.VMEM((heads, count, DV), bf16),
            pltpu.VMEM((n, rows_n, features), f32),
            pltpu.VMEM((rows_n, rows_n * n // 2, features), f32),
            dma((5 + taps,)),
            dma((2, 5)),
            dma((2, 4, 4 * nz)),
            dma((2, n)),
            dma((2, n)),
            dma((2, n)),
            dma((2, 2, n)),
            dma((2, n)),
        ],
        compiler_params=pltpu.CompilerParams(
            collective_id=0, has_side_effects=True, vmem_limit_bytes=60 * 1024 * 1024
        ),
    )(
        signal,
        conv_weight,
        conv_gain.reshape(2, half),
        embed_weight,
        attn_gain.reshape(n, width),
        query_weight,
        keyvalue_weight,
        output_weight,
        rowcol_weight.reshape(n, width, 2 * features),
        pair_weight,
    )
    return jnp.transpose(tokens, (1, 0, 2)).reshape(count // 2, n * width), pair


def fits(mesh):
    n = mesh.shape["seq"]
    return n == 8 and mesh.shape["col"] == 2 and mesh.shape["grp"] == 2


def solution(mesh):
    placed = (
        P(("grp", "seq"), "col"),
        P(None, None, "col"),
        P(),
        P("col", "seq"),
        P(),
        P("seq", None),
        P("seq", None),
        P(None, "seq"),
        P(),
        P(),
    )
    return jax.shard_map(
        on_device_fused if fits(mesh) else on_device,
        mesh=mesh,
        in_specs=placed,
        out_specs=(P(("grp", "seq", "col"), None), P(("grp", "seq"), "col", None)),
        check_vma=False,
    )
```

```python
import functools

import jax
import jax.numpy as jnp
from jax import lax
from jax.experimental import pallas as pl
from jax.experimental.pallas import tpu as pltpu
from jax.sharding import PartitionSpec as P

DK = 128
DV = 192
POOL = 4
PAIR_POOL = 16


def with_halo(array, sides, width):
    for axis, dim in sides:
        size, length = (lax.axis_size(axis), array.shape[dim])
        up = [(i, (i + 1) % size) for i in range(size - 1)]
        down = [(j, i) for i, j in up]
        last = lax.slice_in_dim(array, length - width, length, axis=dim)
        first = lax.slice_in_dim(array, 0, width, axis=dim)
        before = lax.ppermute(last, axis, up)
        after = lax.ppermute(first, axis, down)
        array = jnp.concatenate([before, array, after], axis=dim)
    return array


def rms_scale(values, gain_vector):
    return (
        values * lax.rsqrt(jnp.mean(values * values, axis=-1, keepdims=True) + 1e-06) * gain_vector
    )


def attention_parts(queries, head_count):
    query_rows = queries.reshape(queries.shape[0] * head_count, DK)

    def absorb(running, pieces, first_row):
        running_max, running_sum, accumulated = running
        key_piece, value_piece = pieces
        scores = lax.dot_general(
            query_rows, key_piece, (((1,), (1,)), ((), ())), preferred_element_type=jnp.float32
        )
        newest_max = jnp.maximum(running_max, jnp.max(scores, axis=1))
        weights = jnp.exp(scores - newest_max[:, None])
        running_sum = jnp.sum(weights, axis=1)
        accumulated = jnp.dot(
            weights.astype(jnp.bfloat16), value_piece, preferred_element_type=jnp.float32
        )
        return (newest_max, running_sum, accumulated)

    row_count = query_rows.shape[0]
    initial = (
        jnp.full((row_count,), -1e30, jnp.float32),
        jnp.zeros((row_count,), jnp.float32),
        jnp.zeros((row_count, DV), jnp.float32),
    )
    return (absorb, initial)


def finish_attention(result, token_count):
    running_max, running_sum, accumulated = result
    return (accumulated / running_sum[:, None]).astype(jnp.bfloat16).reshape(token_count, -1)


def on_device(
    signal,
    conv_weight,
    conv_gain,
    embed_weight,
    attn_gain,
    query_weight,
    keyvalue_weight,
    output_weight,
    rowcol_weight,
    pair_weight,
):
    positions = signal.shape[0]
    tap_count = conv_weight.shape[0]
    halo_width = tap_count // 2
    padded = with_halo(signal, (("seq", 0),), halo_width)
    widened = lax.all_gather(padded, "col", axis=1, tiled=True)
    activated = jax.nn.gelu(
        rms_scale(widened.astype(jnp.float32), conv_gain), approximate=True
    ).astype(jnp.bfloat16)
    summed = signal.astype(jnp.float32)
    for tap_index in range(tap_count):
        summed = summed + jnp.dot(
            activated[tap_index : tap_index + positions],
            conv_weight[tap_index],
            preferred_element_type=jnp.float32,
        )
    pooled = jnp.mean(summed.reshape(positions // POOL, POOL, -1), axis=1).astype(jnp.bfloat16)
    embed_full = lax.all_gather(embed_weight, "seq", axis=1, tiled=True)
    col_count = lax.axis_size("col")
    embedded = lax.psum_scatter(
        jnp.dot(pooled, embed_full, preferred_element_type=jnp.float32).astype(jnp.bfloat16),
        "col",
        scatter_dimension=0,
        tiled=True,
    )
    normed = rms_scale(embedded.astype(jnp.float32), attn_gain).astype(jnp.bfloat16)
    head_count = query_weight.shape[1] // DK
    scaling = DK ** (-0.5)
    col_index = lax.axis_index("col")
    local_heads = head_count // col_count
    group_tokens = lax.all_gather(normed, "col", axis=0, tiled=True)
    group_count = group_tokens.shape[0]
    query_half = lax.dynamic_slice_in_dim(
        query_weight, col_index * local_heads * DK, local_heads * DK, 1
    )
    query_sum = jnp.dot(
        group_tokens,
        lax.all_gather(query_half, "seq", axis=0, tiled=True),
        preferred_element_type=jnp.float32,
    )
    keyvalue_sum = jnp.dot(
        group_tokens,
        lax.all_gather(keyvalue_weight, "seq", axis=0, tiled=True),
        preferred_element_type=jnp.float32,
    )
    queries = (query_sum * scaling).astype(jnp.bfloat16)
    keyvalue = keyvalue_sum.astype(jnp.bfloat16)
    absorb, initial = attention_parts(queries, local_heads)
    result = absorb(
        initial,
        (
            lax.all_gather(keyvalue[:, :DK], "seq", axis=0, tiled=True),
            lax.all_gather(keyvalue[:, DK:], "seq", axis=0, tiled=True),
        ),
        jnp.int32(0),
    )
    attended = finish_attention(result, group_count)
    output_half = lax.dynamic_slice_in_dim(
        output_weight, col_index * local_heads * DV, local_heads * DV, 0
    )
    partial_out = jnp.dot(
        attended,
        lax.all_gather(output_half, "seq", axis=1, tiled=True),
        preferred_element_type=jnp.float32,
    )
    attention_out = lax.psum_scatter(
        partial_out.astype(jnp.bfloat16), "col", scatter_dimension=0, tiled=True
    ).astype(jnp.float32)
    tokens = (embedded.astype(jnp.float32) + attention_out).astype(jnp.bfloat16)
    pair_pool = jnp.mean(
        tokens.astype(jnp.float32).reshape(-1, PAIR_POOL, tokens.shape[1]), axis=1
    ).astype(jnp.bfloat16)
    projected = jnp.dot(pair_pool, rowcol_weight, preferred_element_type=jnp.float32).astype(
        jnp.bfloat16
    )
    features = pair_weight.shape[0]
    row_block = lax.all_gather(projected, "col", axis=0, tiled=True)
    column_all = lax.all_gather(row_block[:, features:], "seq", axis=0, tiled=True)
    row_part = row_block[:, :features]
    column_span = column_all.shape[0] // col_count
    column_part = lax.dynamic_slice_in_dim(
        column_all, lax.axis_index("col") * column_span, column_span, 0
    )
    hidden = jax.nn.gelu(
        row_part.astype(jnp.float32)[:, None, :] + column_part.astype(jnp.float32)[None, :, :],
        approximate=True,
    ).astype(jnp.bfloat16)
    pair_out = jnp.dot(
        hidden.reshape(-1, features), pair_weight, preferred_element_type=jnp.float32
    ).astype(jnp.bfloat16)
    return (tokens, pair_out.reshape(row_part.shape[0], column_span, features))


EDGE = 16
Y = 2


def fused_kernel(
    taps,
    heads,
    signal,
    conv_w,
    conv_gain,
    embed_w,
    attn_gain,
    query_w,
    kv_w,
    out_w,
    rowcol,
    pair_w,
    tokens_out,
    pair_out,
    sig,
    act,
    win,
    edge,
    halo,
    conv_buf,
    e_buf,
    q_buf,
    k_buf,
    o_buf,
    part,
    other,
    emb,
    normed,
    kv_all,
    cols,
    hid,
    loc_sem,
    sig_sem,
    w_sem,
    p_sem,
    kv_sem,
    kp_sem,
    ex_sem,
    col_sem,
):
    f32, bf16 = jnp.float32, jnp.bfloat16
    n = lax.axis_size("seq")
    nz = n // Y
    s = lax.axis_index("seq")
    c = lax.axis_index("col")
    x = lax.axis_index("grp")
    z, y = s // Y, s % Y
    half = sig.shape[1]
    positions = sig.shape[2]
    count = positions // POOL
    width = e_buf.shape[1]
    halo_width = taps // 2
    started = []

    def remote(src, dst, sems, index, to):
        copy = pltpu.make_async_remote_copy(
            src_ref=src,
            dst_ref=dst,
            send_sem=sems.at[(0,) + index],
            recv_sem=sems.at[(1,) + index],
            device_id=to,
            device_id_type=pl.DeviceIdType.MESH,
        )
        copy.start()
        started.append(copy)
        return copy

    def seq_of(z_index, y_index):
        return z_index * Y + y_index

    def z_from(dz):
        return (z + nz - dz) % nz

    def z_to(dz):
        return (z + dz) % nz

    partner = {"col": 1 - c}
    y_peer = {"seq": seq_of(z, 1 - y)}
    x_peer = {"grp": 1 - x}

    local = [pltpu.make_async_copy(signal, sig.at[0], loc_sem.at[0])]
    local[0].start()
    k_rows = kv_w.shape[0] // 2
    q_cols = query_w.shape[1] // 2
    o_cols = out_w.shape[1] // 2
    kv_own = kv_w.at[pl.ds(pl.multiple_of(c * k_rows, 16), k_rows)]
    q_own = query_w.at[:, pl.ds(pl.multiple_of(c * q_cols, 128), q_cols)]
    o_own = out_w.at[:, pl.ds(pl.multiple_of(c * o_cols, 128), o_cols)]

    def e_at(owner):
        return e_buf.at[owner]

    def q_at(owner):
        return q_buf.at[owner]

    def k_at(owner, core=None):
        core = c if core is None else core
        return k_buf.at[owner, pl.ds(pl.multiple_of(core * k_rows, 16), k_rows)]

    def o_at(owner):
        return o_buf.at[owner]

    pieces = [(embed_w, e_at), (kv_own, k_at), (q_own, q_at), (o_own, o_at)]
    E, KV, Q, O = range(4)
    whole = (O,)
    for t in range(taps):
        local.append(pltpu.make_async_copy(conv_w.at[t], conv_buf.at[t], loc_sem.at[1 + t]))
    for w, (own, at) in enumerate(pieces):
        local.append(pltpu.make_async_copy(own, at(s), loc_sem.at[1 + taps + w]))
    for copy in local[1:]:
        copy.start()

    barrier = pltpu.get_barrier_semaphore()
    for d in range(n):
        for e in range(2):
            if d or e:
                pl.semaphore_signal(
                    barrier,
                    inc=1,
                    device_id={"seq": (s + d) % n, "col": (c + e) % 2},
                    device_id_type=pl.DeviceIdType.MESH,
                )
    pl.semaphore_signal(barrier, inc=1, device_id=x_peer, device_id_type=pl.DeviceIdType.MESH)
    pl.semaphore_wait(barrier, 2 * n)

    signal_copies = [remote(signal, sig.at[1], sig_sem, (0,), partner)]

    def rows_half(ref, h):
        rows = ref.shape[0] // 2
        return ref.at[pl.ds(pl.multiple_of(h * rows, 16), rows)]

    copies = {}

    def send(w, key, slot, src, dst, to):
        copies[w, key] = remote(src, dst, w_sem, (w, slot), to)

    def along_z(w):
        own, at = pieces[w]
        for dz in range(1, nz):
            to = {"seq": seq_of(z_to(dz), y)}
            if w in whole:
                send(w, ("z", dz), dz, own, at(s), to)
            else:
                send(w, ("z", dz), dz, rows_half(own, x), rows_half(at(s), x), to)

    def own_y(w):
        own, at = pieces[w]
        send(w, ("y", 0), 0, own, at(s), y_peer)

    def stage2(w):
        _, at = pieces[w]
        for dz in range(1, nz):
            copies[w, ("z", dz)].wait_recv()
            ref = rows_half(at(seq_of(z_from(dz), y)), x)
            send(w, ("y", dz), nz + dz, ref, ref, y_peer)
            if w not in whole:
                send(w, ("x", dz), 2 * nz + dz, ref, ref, x_peer)

    def stage3(w):
        _, at = pieces[w]
        for dz in range(1, nz):
            copies[w, ("y", dz)].wait_recv()
            ref = rows_half(at(seq_of(z_from(dz), 1 - y)), x)
            send(w, ("xy", dz), 3 * nz + dz, ref, ref, x_peer)

    def owners():
        order = [(0, True), (0, False)]
        for dz in range(1, nz):
            order += [(dz, True), (dz, False)]
        return order

    def owner_of(dz, same):
        return seq_of(z_from(dz), y if same else 1 - y)

    def arrived(w, dz, same):
        if dz == 0:
            if same:
                local[1 + taps + w].wait()
            else:
                copies[w, ("y", 0)].wait_recv()
        elif not same:
            copies[w, ("xy", dz)].wait_recv()
        elif w not in whole:
            copies[w, ("x", dz)].wait_recv()

    along_z(E)
    own_y(E)
    along_z(KV)
    along_z(Q)
    along_z(O)

    row = lax.broadcasted_iota(jnp.int32, (EDGE, positions), 0)
    place = lax.broadcasted_iota(jnp.int32, (EDGE, positions), 1)
    wanted = jnp.where(row < EDGE // 2, row, row - EDGE // 2 + positions - halo_width)
    in_use = lax.rem(row, EDGE // 2) < halo_width
    pick = jnp.where((place == wanted) & in_use, 1.0, 0.0).astype(bf16)
    local[0].wait()
    over_rows = (((1,), (1,)), ((), ()))
    edge[...] = lax.dot_general(pick, sig[0], over_rows, preferred_element_type=f32).astype(bf16)
    for e in range(2):
        core = (c + e) % 2
        up = {"seq": (s + 1) % n, "col": core}
        down = {"seq": (s + n - 1) % n, "col": core}
        signal_copies.append(remote(edge, halo.at[e, 0], sig_sem, (1 + 2 * e,), up))
        signal_copies.append(remote(edge, halo.at[e, 1], sig_sem, (2 + 2 * e,), down))

    def windows(position):
        column = lax.broadcasted_iota(jnp.int32, position.shape, 1)
        tap = column // count
        begin = (column - tap * count) * POOL + tap - halo_width
        hit = (position >= begin) & (position < begin + POOL)
        return jnp.where(hit, 1.0 / POOL, 0.0).astype(bf16)

    mean_of = windows(lax.broadcasted_iota(jnp.int32, (positions, taps * count), 0))
    edge_row = lax.broadcasted_iota(jnp.int32, (EDGE, taps * count), 0)
    edge_means = [windows(edge_row - EDGE // 2 - halo_width), windows(edge_row + positions)]
    edge_means = [
        jnp.where((edge_row >= EDGE // 2) & (s > 0), edge_means[0], 0.0).astype(bf16),
        jnp.where((edge_row < EDGE // 2) & (s < n - 1), edge_means[1], 0.0).astype(bf16),
    ]
    channels = 2 * half
    gains = [conv_gain[pl.ds(c, 1), :], conv_gain[pl.ds(1 - c, 1), :]]
    gain_columns = [jnp.broadcast_to(g, (128, half)).T for g in gains]

    for copy in signal_copies:
        copy.wait_recv()

    block = 64
    square = jnp.zeros((1, positions), f32)
    for h in range(2):
        v = sig[h].astype(f32)
        square = square + jnp.sum(v * v, axis=0, keepdims=True)
    scale = lax.rsqrt(square * (1.0 / channels) + 1e-06)
    for h in range(2):
        for i in range(half // block):
            rows = slice(i * block, (i + 1) * block)
            v = sig[h, rows, :].astype(f32) * scale * gain_columns[h][rows, :1]
            act[h, rows, :] = jax.nn.gelu(v, approximate=True).astype(bf16)

    edges = [[], []]
    for side in range(2):
        a, b = halo[0, side].astype(f32), halo[1, side].astype(f32)
        ssq = jnp.sum(a * a, axis=1, keepdims=True) + jnp.sum(b * b, axis=1, keepdims=True)
        edge_scale = lax.rsqrt(ssq * (1.0 / channels) + 1e-06)
        for h, v in enumerate((a, b)):
            v = jax.nn.gelu(v * edge_scale * gains[h], approximate=True)
            edges[h].append(v.T.astype(bf16))
    for h in range(2):
        core = c if h == 0 else 1 - c
        mean = jnp.dot(act[h], mean_of, preferred_element_type=f32)
        for side in range(2):
            mean = mean + jnp.dot(edges[h][side], edge_means[side], preferred_element_type=f32)
        win[pl.ds(pl.multiple_of(core * half, 16), half), :] = mean.astype(bf16)

    stage2(E)
    own_y(KV)
    own_y(Q)

    middle = slice(halo_width * count, (halo_width + 1) * count)
    total = jnp.dot(sig[0], mean_of[:, middle], preferred_element_type=f32)
    for t in range(taps):
        local[1 + t].wait()
        total = total + jnp.dot(
            conv_buf[t], win[:, t * count : (t + 1) * count], preferred_element_type=f32
        )
    pooled = total.astype(bf16)

    stage2(KV)
    stage3(E)

    swaps = []
    for k, (dz, same) in enumerate(owners()):
        owner = owner_of(dz, same)
        arrived(E, dz, same)
        part[0, owner] = jnp.dot(e_buf[owner], pooled, preferred_element_type=f32).astype(bf16)
        swaps.append(remote(part.at[0, owner], other.at[0, owner], ex_sem, (0, k), partner))
    stage2(Q)
    own_y(O)
    for copy in swaps:
        copy.wait_recv()
    square = jnp.zeros((1, count), f32)
    for b in range(n):
        v = (part[0, b].astype(f32) + other[0, b].astype(f32)).astype(bf16)
        emb[b] = v
        v = v.astype(f32)
        square = square + jnp.sum(v * v, axis=0, keepdims=True)
    scale = lax.rsqrt(square * (1.0 / (n * width)) + 1e-06)
    for b in range(0, n, 2):
        columns = slice(b * width, (b + 2) * width)
        v = jnp.concatenate([emb[b], emb[b + 1]], axis=0).astype(f32) * scale
        normed[:, columns] = (v.T * attn_gain[:, columns]).astype(bf16)

    stage3(KV)
    stage3(Q)

    passed = []
    for k, (dz, same) in enumerate(owners()):
        arrived(KV, dz, same)
        ref = k_at(owner_of(dz, same))
        passed.append(remote(ref, ref, p_sem, (k,), partner))
    for copy in passed:
        copy.wait_recv()
    own_tokens = pl.ds(pl.multiple_of(c * (count // 2), 16), count // 2)
    kv = jnp.dot(
        normed[own_tokens, :],
        k_buf[...].reshape(n * width, k_buf.shape[2]),
        preferred_element_type=f32,
    )

    def kv_at(owner):
        return kv_all.at[owner, own_tokens]

    kv_all[s, own_tokens, :] = kv.astype(bf16)
    mine = kv_at(s)
    kv_copies = {}
    for dz in range(1, nz):
        to = {"seq": seq_of(z_to(dz), y)}
        kv_copies["z", dz] = remote(mine, mine, kv_sem, (dz,), to)
    kv_copies["y", 0] = remote(mine, mine, kv_sem, (0,), y_peer)
    across = [remote(mine, mine, kp_sem, (0,), partner)]

    for dz, same in owners():
        arrived(Q, dz, same)
    queries = jnp.dot(
        normed[...], q_buf[...].reshape(n * width, q_cols), preferred_element_type=f32
    )
    queries = (queries * (DK**-0.5)).astype(bf16)

    for dz in range(1, nz):
        kv_copies["z", dz].wait_recv()
        ref = kv_at(seq_of(z_from(dz), y))
        kv_copies["y", dz] = remote(ref, ref, kv_sem, (nz + dz,), y_peer)
        across.append(remote(ref, ref, kp_sem, (dz,), partner))
    stage2(O)
    for dz in range(nz):
        kv_copies["y", dz].wait_recv()
        ref = kv_at(seq_of(z_from(dz), 1 - y))
        across.append(remote(ref, ref, kp_sem, (nz + dz,), partner))
    for copy in across:
        copy.wait_recv()

    everything = kv_all[...].reshape(n * count, kv_all.shape[2])
    keys, values = everything[:, :DK], everything[:, DK:]
    att = []
    for h in range(heads):
        scores = lax.dot_general(
            queries[:, h * DK : (h + 1) * DK],
            keys,
            (((1,), (1,)), ((), ())),
            preferred_element_type=f32,
        )
        weights = jnp.exp(scores - jnp.max(scores, axis=1, keepdims=True))
        norm = jnp.sum(weights, axis=1, keepdims=True)
        mixed = jnp.dot(weights.astype(bf16), values, preferred_element_type=f32)
        att.append((mixed / norm).astype(bf16))
    att = jnp.concatenate(att, axis=1)

    stage3(O)
    swaps = []
    for k, (dz, same) in enumerate(owners()):
        owner = owner_of(dz, same)
        arrived(O, dz, same)
        acc = lax.dot_general(o_buf[owner], att, over_rows, preferred_element_type=f32)
        part[1, owner] = acc.astype(bf16)
        swaps.append(remote(part.at[1, owner], other.at[1, owner], ex_sem, (1, k), partner))
    for copy in swaps:
        copy.wait_recv()

    rows_n = count // PAIR_POOL
    row_of = lax.broadcasted_iota(jnp.int32, (rows_n, count), 0)
    token_of = lax.broadcasted_iota(jnp.int32, (rows_n, count), 1) // PAIR_POOL
    pool = jnp.where(row_of == token_of, 1.0 / PAIR_POOL, 0.0).astype(bf16)
    features = pair_w.shape[0]
    for b in range(0, n, 2):
        columns = slice(b * width, (b + 2) * width)
        pair = [
            emb[k].astype(f32) + (part[1, k].astype(f32) + other[1, k].astype(f32))
            for k in (b, b + 1)
        ]
        normed[:, columns] = jnp.concatenate(pair, axis=0).T.astype(bf16)
    pair_pool = jnp.dot(pool, normed[...], preferred_element_type=f32).astype(bf16)
    projected = jnp.dot(pair_pool, rowcol[...], preferred_element_type=f32)
    projected = projected.astype(bf16).astype(f32)
    cols[s] = projected[:, features:]
    col_copies = []
    for d in range(1, n):
        to = {"seq": (s + d) % n}
        col_copies.append(remote(cols.at[s], cols.at[s], col_sem, (d,), to))
    tokens_out[...] = normed[own_tokens, :]
    for copy in col_copies:
        copy.wait_recv()
    row_part = projected[:, None, :features]
    for j in range(n // 2):
        column = cols[c * (n // 2) + j]
        hid[:, pl.ds(j * rows_n, rows_n), :] = jax.nn.gelu(
            row_part + column[None, :, :], approximate=True
        )
    hidden = hid[...].reshape(rows_n * (n // 2) * rows_n, features).astype(bf16)
    result = jnp.dot(hidden, pair_w[...], preferred_element_type=f32)
    pair_out[...] = result.reshape(pair_out.shape).astype(bf16)
    for copy in started:
        copy.wait_send()


def on_device_fused(
    signal,
    conv_weight,
    conv_gain,
    embed_weight,
    attn_gain,
    query_weight,
    keyvalue_weight,
    output_weight,
    rowcol_weight,
    pair_weight,
):
    bf16, f32 = jnp.bfloat16, jnp.float32
    n = lax.axis_size("seq")
    nz = n // Y
    positions, half = signal.shape
    taps, channels, _ = conv_weight.shape
    count = positions // POOL
    width = embed_weight.shape[1]
    q_cols = query_weight.shape[1] // 2
    heads = q_cols // DK
    kv_cols = keyvalue_weight.shape[1]
    rows_n = count // PAIR_POOL
    features = pair_weight.shape[0]
    any_spec = pl.BlockSpec(memory_space=pl.ANY)
    vmem = pl.BlockSpec(memory_space=pltpu.VMEM)
    dma = pltpu.SemaphoreType.DMA
    tokens, pair = pl.pallas_call(
        functools.partial(fused_kernel, taps, heads),
        out_shape=(
            jax.ShapeDtypeStruct((count // 2, n * width), bf16),
            jax.ShapeDtypeStruct((rows_n, rows_n * n // 2, features), bf16),
        ),
        in_specs=[any_spec, any_spec, vmem, any_spec, vmem]
        + [any_spec, any_spec, any_spec, vmem, vmem],
        out_specs=(vmem, vmem),
        scratch_shapes=[
            pltpu.VMEM((2, half, positions), bf16),
            pltpu.VMEM((2, half, positions), bf16),
            pltpu.VMEM((2 * half, taps * count), bf16),
            pltpu.VMEM((EDGE, half), bf16),
            pltpu.VMEM((2, 2, EDGE, half), bf16),
            pltpu.VMEM((taps, half, channels), bf16),
            pltpu.VMEM((n, width, half), bf16),
            pltpu.VMEM((n, width, q_cols), bf16),
            pltpu.VMEM((n, width, kv_cols), bf16),
            pltpu.VMEM((n, width, heads * DV), bf16),
            pltpu.VMEM((2, n, width, count), bf16),
            pltpu.VMEM((2, n, width, count), bf16),
            pltpu.VMEM((n, width, count), bf16),
            pltpu.VMEM((count, n * width), bf16),
            pltpu.VMEM((n, count, kv_cols), bf16),
            pltpu.VMEM((n, rows_n, features), f32),
            pltpu.VMEM((rows_n, rows_n * n // 2, features), f32),
            dma((5 + taps,)),
            dma((2, 5)),
            dma((2, 4, 4 * nz)),
            dma((2, n)),
            dma((2, n)),
            dma((2, n)),
            dma((2, 2, n)),
            dma((2, n)),
        ],
        compiler_params=pltpu.CompilerParams(
            collective_id=0, has_side_effects=True, vmem_limit_bytes=60 * 1024 * 1024
        ),
    )(
        signal.T,
        jnp.swapaxes(conv_weight, 1, 2),
        conv_gain.reshape(2, half),
        embed_weight.T,
        attn_gain.reshape(1, n * width),
        query_weight,
        keyvalue_weight,
        output_weight.T,
        rowcol_weight,
        pair_weight,
    )
    return tokens, pair


def fits(mesh):
    n = mesh.shape["seq"]
    return n == 8 and mesh.shape["col"] == 2 and mesh.shape["grp"] == 2


def solution(mesh):
    placed = (
        P(("grp", "seq"), "col"),
        P(None, None, "col"),
        P(),
        P("col", "seq"),
        P(),
        P("seq", None),
        P("seq", None),
        P(None, "seq"),
        P(),
        P(),
    )
    return jax.shard_map(
        on_device_fused if fits(mesh) else on_device,
        mesh=mesh,
        in_specs=placed,
        out_specs=(P(("grp", "seq", "col"), None), P(("grp", "seq"), "col", None)),
        check_vma=False,
    )
```

```python
import functools

import jax
import jax.numpy as jnp
from jax import lax
from jax.experimental import pallas as pl
from jax.experimental.pallas import tpu as pltpu
from jax.sharding import PartitionSpec as P

DK = 128
DV = 192
POOL = 4
PAIR_POOL = 16


def with_halo(array, sides, width):
    for axis, dim in sides:
        size, length = (lax.axis_size(axis), array.shape[dim])
        up = [(i, (i + 1) % size) for i in range(size - 1)]
        down = [(j, i) for i, j in up]
        last = lax.slice_in_dim(array, length - width, length, axis=dim)
        first = lax.slice_in_dim(array, 0, width, axis=dim)
        before = lax.ppermute(last, axis, up)
        after = lax.ppermute(first, axis, down)
        array = jnp.concatenate([before, array, after], axis=dim)
    return array


def rms_scale(values, gain_vector):
    return (
        values * lax.rsqrt(jnp.mean(values * values, axis=-1, keepdims=True) + 1e-06) * gain_vector
    )


def attention_parts(queries, head_count):
    query_rows = queries.reshape(queries.shape[0] * head_count, DK)

    def absorb(running, pieces, first_row):
        running_max, running_sum, accumulated = running
        key_piece, value_piece = pieces
        scores = lax.dot_general(
            query_rows, key_piece, (((1,), (1,)), ((), ())), preferred_element_type=jnp.float32
        )
        newest_max = jnp.maximum(running_max, jnp.max(scores, axis=1))
        weights = jnp.exp(scores - newest_max[:, None])
        running_sum = jnp.sum(weights, axis=1)
        accumulated = jnp.dot(
            weights.astype(jnp.bfloat16), value_piece, preferred_element_type=jnp.float32
        )
        return (newest_max, running_sum, accumulated)

    row_count = query_rows.shape[0]
    initial = (
        jnp.full((row_count,), -1e30, jnp.float32),
        jnp.zeros((row_count,), jnp.float32),
        jnp.zeros((row_count, DV), jnp.float32),
    )
    return (absorb, initial)


def finish_attention(result, token_count):
    running_max, running_sum, accumulated = result
    return (accumulated / running_sum[:, None]).astype(jnp.bfloat16).reshape(token_count, -1)


def on_device(
    signal,
    conv_weight,
    conv_gain,
    embed_weight,
    attn_gain,
    query_weight,
    keyvalue_weight,
    output_weight,
    rowcol_weight,
    pair_weight,
):
    positions = signal.shape[0]
    tap_count = conv_weight.shape[0]
    halo_width = tap_count // 2
    padded = with_halo(signal, (("seq", 0),), halo_width)
    widened = lax.all_gather(padded, "col", axis=1, tiled=True)
    activated = jax.nn.gelu(
        rms_scale(widened.astype(jnp.float32), conv_gain), approximate=True
    ).astype(jnp.bfloat16)
    summed = signal.astype(jnp.float32)
    for tap_index in range(tap_count):
        summed = summed + jnp.dot(
            activated[tap_index : tap_index + positions],
            conv_weight[tap_index],
            preferred_element_type=jnp.float32,
        )
    pooled = jnp.mean(summed.reshape(positions // POOL, POOL, -1), axis=1).astype(jnp.bfloat16)
    embed_full = lax.all_gather(embed_weight, "seq", axis=1, tiled=True)
    col_count = lax.axis_size("col")
    embedded = lax.psum_scatter(
        jnp.dot(pooled, embed_full, preferred_element_type=jnp.float32).astype(jnp.bfloat16),
        "col",
        scatter_dimension=0,
        tiled=True,
    )
    normed = rms_scale(embedded.astype(jnp.float32), attn_gain).astype(jnp.bfloat16)
    head_count = query_weight.shape[1] // DK
    scaling = DK ** (-0.5)
    col_index = lax.axis_index("col")
    local_heads = head_count // col_count
    group_tokens = lax.all_gather(normed, "col", axis=0, tiled=True)
    group_count = group_tokens.shape[0]
    query_half = lax.dynamic_slice_in_dim(
        query_weight, col_index * local_heads * DK, local_heads * DK, 1
    )
    query_sum = jnp.dot(
        group_tokens,
        lax.all_gather(query_half, "seq", axis=0, tiled=True),
        preferred_element_type=jnp.float32,
    )
    keyvalue_sum = jnp.dot(
        group_tokens,
        lax.all_gather(keyvalue_weight, "seq", axis=0, tiled=True),
        preferred_element_type=jnp.float32,
    )
    queries = (query_sum * scaling).astype(jnp.bfloat16)
    keyvalue = keyvalue_sum.astype(jnp.bfloat16)
    absorb, initial = attention_parts(queries, local_heads)
    result = absorb(
        initial,
        (
            lax.all_gather(keyvalue[:, :DK], "seq", axis=0, tiled=True),
            lax.all_gather(keyvalue[:, DK:], "seq", axis=0, tiled=True),
        ),
        jnp.int32(0),
    )
    attended = finish_attention(result, group_count)
    output_half = lax.dynamic_slice_in_dim(
        output_weight, col_index * local_heads * DV, local_heads * DV, 0
    )
    partial_out = jnp.dot(
        attended,
        lax.all_gather(output_half, "seq", axis=1, tiled=True),
        preferred_element_type=jnp.float32,
    )
    attention_out = lax.psum_scatter(
        partial_out.astype(jnp.bfloat16), "col", scatter_dimension=0, tiled=True
    ).astype(jnp.float32)
    tokens = (embedded.astype(jnp.float32) + attention_out).astype(jnp.bfloat16)
    pair_pool = jnp.mean(
        tokens.astype(jnp.float32).reshape(-1, PAIR_POOL, tokens.shape[1]), axis=1
    ).astype(jnp.bfloat16)
    projected = jnp.dot(pair_pool, rowcol_weight, preferred_element_type=jnp.float32).astype(
        jnp.bfloat16
    )
    features = pair_weight.shape[0]
    row_block = lax.all_gather(projected, "col", axis=0, tiled=True)
    column_all = lax.all_gather(row_block[:, features:], "seq", axis=0, tiled=True)
    row_part = row_block[:, :features]
    column_span = column_all.shape[0] // col_count
    column_part = lax.dynamic_slice_in_dim(
        column_all, lax.axis_index("col") * column_span, column_span, 0
    )
    hidden = jax.nn.gelu(
        row_part.astype(jnp.float32)[:, None, :] + column_part.astype(jnp.float32)[None, :, :],
        approximate=True,
    ).astype(jnp.bfloat16)
    pair_out = jnp.dot(
        hidden.reshape(-1, features), pair_weight, preferred_element_type=jnp.float32
    ).astype(jnp.bfloat16)
    return (tokens, pair_out.reshape(row_part.shape[0], column_span, features))


EDGE = 16
Y = 2


def fused_kernel(
    taps,
    heads,
    signal,
    conv_w,
    conv_gain,
    embed_w,
    attn_gain,
    query_w,
    kv_w,
    out_w,
    rowcol,
    pair_w,
    tokens_out,
    pair_out,
    sig,
    act,
    win,
    edge,
    halo,
    conv_buf,
    e_buf,
    q_buf,
    k_buf,
    o_buf,
    part,
    other,
    emb,
    normed,
    kv_all,
    cols,
    hid,
    loc_sem,
    sig_sem,
    w_sem,
    p_sem,
    kv_sem,
    kp_sem,
    ex_sem,
    col_sem,
):
    f32, bf16 = jnp.float32, jnp.bfloat16
    n = lax.axis_size("seq")
    nz = n // Y
    s = lax.axis_index("seq")
    c = lax.axis_index("col")
    x = lax.axis_index("grp")
    z, y = s // Y, s % Y
    half = sig.shape[1]
    positions = sig.shape[2]
    count = positions // POOL
    width = e_buf.shape[1]
    halo_width = taps // 2
    started = []

    def remote(src, dst, sems, index, to):
        copy = pltpu.make_async_remote_copy(
            src_ref=src,
            dst_ref=dst,
            send_sem=sems.at[(0,) + index],
            recv_sem=sems.at[(1,) + index],
            device_id=to,
            device_id_type=pl.DeviceIdType.MESH,
        )
        copy.start()
        started.append(copy)
        return copy

    def seq_of(z_index, y_index):
        return z_index * Y + y_index

    def z_from(dz):
        return (z + nz - dz) % nz

    def z_to(dz):
        return (z + dz) % nz

    partner = {"col": 1 - c}
    y_peer = {"seq": seq_of(z, 1 - y)}
    x_peer = {"grp": 1 - x}
    z_next = {"seq": seq_of(z_to(1), y)}

    local = [pltpu.make_async_copy(signal, sig.at[0], loc_sem.at[0])]
    local[0].start()
    k_rows = kv_w.shape[0] // 2
    q_cols = query_w.shape[1] // 2
    o_cols = out_w.shape[1] // 2
    kv_own = kv_w.at[pl.ds(pl.multiple_of(c * k_rows, 16), k_rows)]
    q_own = query_w.at[:, pl.ds(pl.multiple_of(c * q_cols, 128), q_cols)]
    o_own = out_w.at[:, pl.ds(pl.multiple_of(c * o_cols, 128), o_cols)]

    def e_at(owner):
        return e_buf.at[owner]

    def q_at(owner):
        return q_buf.at[owner]

    def k_at(owner, core=None):
        core = c if core is None else core
        return k_buf.at[owner, pl.ds(pl.multiple_of(core * k_rows, 16), k_rows)]

    def o_at(owner):
        return o_buf.at[owner]

    pieces = [(embed_w, e_at), (kv_own, k_at), (q_own, q_at), (o_own, o_at)]
    E, KV, Q, O = range(4)
    for t in range(taps):
        local.append(pltpu.make_async_copy(conv_w.at[t], conv_buf.at[t], loc_sem.at[1 + t]))
    for w, (own, at) in enumerate(pieces):
        local.append(pltpu.make_async_copy(own, at(s), loc_sem.at[1 + taps + w]))
    for copy in local[1:]:
        copy.start()

    barrier = pltpu.get_barrier_semaphore()
    for d in range(n):
        for e in range(2):
            if d or e:
                pl.semaphore_signal(
                    barrier,
                    inc=1,
                    device_id={"seq": (s + d) % n, "col": (c + e) % 2},
                    device_id_type=pl.DeviceIdType.MESH,
                )
    pl.semaphore_signal(barrier, inc=1, device_id=x_peer, device_id_type=pl.DeviceIdType.MESH)
    pl.semaphore_wait(barrier, 2 * n)

    signal_copies = [remote(signal, sig.at[1], sig_sem, (0,), partner)]

    def rows_half(ref, h):
        rows = ref.shape[0] // 2
        return ref.at[pl.ds(pl.multiple_of(h * rows, 16), rows)]

    copies = {}

    def send(w, key, slot, src, dst, to):
        copies[w, key] = remote(src, dst, w_sem, (w, slot), to)

    def along_z(w):
        own, at = pieces[w]
        send(w, ("z", 1), 1, rows_half(own, x), rows_half(at(s), x), z_next)

    def own_y(w):
        own, at = pieces[w]
        send(w, ("y", 0), 0, own, at(s), y_peer)

    def stage2(w):
        _, at = pieces[w]
        for dz in range(1, nz):
            copies[w, ("z", dz)].wait_recv()
            ref = rows_half(at(seq_of(z_from(dz), y)), x)
            if dz + 1 < nz:
                send(w, ("z", dz + 1), dz + 1, ref, ref, z_next)
            send(w, ("y", dz), nz + dz, ref, ref, y_peer)
            send(w, ("x", dz), 2 * nz + dz, ref, ref, x_peer)

    def stage3(w):
        _, at = pieces[w]
        for dz in range(1, nz):
            copies[w, ("y", dz)].wait_recv()
            ref = rows_half(at(seq_of(z_from(dz), 1 - y)), x)
            send(w, ("xy", dz), 3 * nz + dz, ref, ref, x_peer)

    def owners():
        order = [(0, True), (0, False)]
        for dz in range(1, nz):
            order += [(dz, True), (dz, False)]
        return order

    def owner_of(dz, same):
        return seq_of(z_from(dz), y if same else 1 - y)

    def arrived(w, dz, same):
        if dz == 0:
            if same:
                local[1 + taps + w].wait()
            else:
                copies[w, ("y", 0)].wait_recv()
        elif not same:
            copies[w, ("xy", dz)].wait_recv()
        else:
            copies[w, ("x", dz)].wait_recv()

    along_z(E)
    own_y(E)
    along_z(KV)
    along_z(Q)
    along_z(O)

    row = lax.broadcasted_iota(jnp.int32, (EDGE, positions), 0)
    place = lax.broadcasted_iota(jnp.int32, (EDGE, positions), 1)
    wanted = jnp.where(row < EDGE // 2, row, row - EDGE // 2 + positions - halo_width)
    in_use = lax.rem(row, EDGE // 2) < halo_width
    pick = jnp.where((place == wanted) & in_use, 1.0, 0.0).astype(bf16)
    local[0].wait()
    over_rows = (((1,), (1,)), ((), ()))
    edge[...] = lax.dot_general(pick, sig[0], over_rows, preferred_element_type=f32).astype(bf16)
    for e in range(2):
        core = (c + e) % 2
        up = {"seq": (s + 1) % n, "col": core}
        down = {"seq": (s + n - 1) % n, "col": core}
        signal_copies.append(remote(edge, halo.at[e, 0], sig_sem, (1 + 2 * e,), up))
        signal_copies.append(remote(edge, halo.at[e, 1], sig_sem, (2 + 2 * e,), down))

    def windows(position):
        column = lax.broadcasted_iota(jnp.int32, position.shape, 1)
        tap = column // count
        begin = (column - tap * count) * POOL + tap - halo_width
        hit = (position >= begin) & (position < begin + POOL)
        return jnp.where(hit, 1.0 / POOL, 0.0).astype(bf16)

    mean_of = windows(lax.broadcasted_iota(jnp.int32, (positions, taps * count), 0))
    edge_row = lax.broadcasted_iota(jnp.int32, (EDGE, taps * count), 0)
    edge_means = [windows(edge_row - EDGE // 2 - halo_width), windows(edge_row + positions)]
    edge_means = [
        jnp.where((edge_row >= EDGE // 2) & (s > 0), edge_means[0], 0.0).astype(bf16),
        jnp.where((edge_row < EDGE // 2) & (s < n - 1), edge_means[1], 0.0).astype(bf16),
    ]
    channels = 2 * half
    gains = [conv_gain[pl.ds(c, 1), :], conv_gain[pl.ds(1 - c, 1), :]]
    gain_columns = [jnp.broadcast_to(g, (128, half)).T for g in gains]

    for copy in signal_copies:
        copy.wait_recv()

    block = 64
    square = jnp.zeros((1, positions), f32)
    for h in range(2):
        v = sig[h].astype(f32)
        square = square + jnp.sum(v * v, axis=0, keepdims=True)
    scale = lax.rsqrt(square * (1.0 / channels) + 1e-06)
    for h in range(2):
        for i in range(half // block):
            rows = slice(i * block, (i + 1) * block)
            v = sig[h, rows, :].astype(f32) * scale * gain_columns[h][rows, :1]
            act[h, rows, :] = jax.nn.gelu(v, approximate=True).astype(bf16)

    edges = [[], []]
    for side in range(2):
        a, b = halo[0, side].astype(f32), halo[1, side].astype(f32)
        ssq = jnp.sum(a * a, axis=1, keepdims=True) + jnp.sum(b * b, axis=1, keepdims=True)
        edge_scale = lax.rsqrt(ssq * (1.0 / channels) + 1e-06)
        for h, v in enumerate((a, b)):
            v = jax.nn.gelu(v * edge_scale * gains[h], approximate=True)
            edges[h].append(v.T.astype(bf16))
    for h in range(2):
        core = c if h == 0 else 1 - c
        mean = jnp.dot(act[h], mean_of, preferred_element_type=f32)
        for side in range(2):
            mean = mean + jnp.dot(edges[h][side], edge_means[side], preferred_element_type=f32)
        win[pl.ds(pl.multiple_of(core * half, 16), half), :] = mean.astype(bf16)

    stage2(E)
    own_y(KV)
    own_y(Q)

    middle = slice(halo_width * count, (halo_width + 1) * count)
    total = jnp.dot(sig[0], mean_of[:, middle], preferred_element_type=f32)
    for t in range(taps):
        local[1 + t].wait()
        total = total + jnp.dot(
            conv_buf[t], win[:, t * count : (t + 1) * count], preferred_element_type=f32
        )
    pooled = total.astype(bf16)

    stage2(KV)
    stage3(E)

    swaps = []
    for k, (dz, same) in enumerate(owners()):
        owner = owner_of(dz, same)
        arrived(E, dz, same)
        part[0, owner] = jnp.dot(e_buf[owner], pooled, preferred_element_type=f32).astype(bf16)
        swaps.append(remote(part.at[0, owner], other.at[0, owner], ex_sem, (0, k), partner))
    stage2(Q)
    own_y(O)
    for copy in swaps:
        copy.wait_recv()
    square = jnp.zeros((1, count), f32)
    for b in range(n):
        v = (part[0, b].astype(f32) + other[0, b].astype(f32)).astype(bf16)
        emb[b] = v
        v = v.astype(f32)
        square = square + jnp.sum(v * v, axis=0, keepdims=True)
    scale = lax.rsqrt(square * (1.0 / (n * width)) + 1e-06)
    for b in range(0, n, 2):
        columns = slice(b * width, (b + 2) * width)
        v = jnp.concatenate([emb[b], emb[b + 1]], axis=0).astype(f32) * scale
        normed[:, columns] = (v.T * attn_gain[:, columns]).astype(bf16)

    stage3(KV)
    stage3(Q)

    passed = []
    for k, (dz, same) in enumerate(owners()):
        arrived(KV, dz, same)
        ref = k_at(owner_of(dz, same))
        passed.append(remote(ref, ref, p_sem, (k,), partner))
    for copy in passed:
        copy.wait_recv()
    own_tokens = pl.ds(pl.multiple_of(c * (count // 2), 16), count // 2)
    kv = jnp.dot(
        normed[own_tokens, :],
        k_buf[...].reshape(n * width, k_buf.shape[2]),
        preferred_element_type=f32,
    )

    def kv_at(owner):
        return kv_all.at[owner, own_tokens]

    kv_all[s, own_tokens, :] = kv.astype(bf16)
    mine = kv_at(s)
    kv_copies = {}
    for dz in range(1, nz):
        to = {"seq": seq_of(z_to(dz), y)}
        kv_copies["z", dz] = remote(mine, mine, kv_sem, (dz,), to)
    kv_copies["y", 0] = remote(mine, mine, kv_sem, (0,), y_peer)
    across = [remote(mine, mine, kp_sem, (0,), partner)]

    for dz, same in owners():
        arrived(Q, dz, same)
    queries = jnp.dot(
        normed[...], q_buf[...].reshape(n * width, q_cols), preferred_element_type=f32
    )
    queries = (queries * (DK**-0.5)).astype(bf16)

    for dz in range(1, nz):
        kv_copies["z", dz].wait_recv()
        ref = kv_at(seq_of(z_from(dz), y))
        kv_copies["y", dz] = remote(ref, ref, kv_sem, (nz + dz,), y_peer)
        across.append(remote(ref, ref, kp_sem, (dz,), partner))
    stage2(O)
    for dz in range(nz):
        kv_copies["y", dz].wait_recv()
        ref = kv_at(seq_of(z_from(dz), 1 - y))
        across.append(remote(ref, ref, kp_sem, (nz + dz,), partner))
    for copy in across:
        copy.wait_recv()

    everything = kv_all[...].reshape(n * count, kv_all.shape[2])
    keys, values = everything[:, :DK], everything[:, DK:]
    att = []
    for h in range(heads):
        scores = lax.dot_general(
            queries[:, h * DK : (h + 1) * DK],
            keys,
            (((1,), (1,)), ((), ())),
            preferred_element_type=f32,
        )
        weights = jnp.exp(scores - jnp.max(scores, axis=1, keepdims=True))
        norm = jnp.sum(weights, axis=1, keepdims=True)
        mixed = jnp.dot(weights.astype(bf16), values, preferred_element_type=f32)
        att.append((mixed / norm).astype(bf16))
    att = jnp.concatenate(att, axis=1)

    stage3(O)
    swaps = []
    for k, (dz, same) in enumerate(owners()):
        owner = owner_of(dz, same)
        arrived(O, dz, same)
        acc = lax.dot_general(o_buf[owner], att, over_rows, preferred_element_type=f32)
        part[1, owner] = acc.astype(bf16)
        swaps.append(remote(part.at[1, owner], other.at[1, owner], ex_sem, (1, k), partner))
    for copy in swaps:
        copy.wait_recv()

    rows_n = count // PAIR_POOL
    row_of = lax.broadcasted_iota(jnp.int32, (rows_n, count), 0)
    token_of = lax.broadcasted_iota(jnp.int32, (rows_n, count), 1) // PAIR_POOL
    pool = jnp.where(row_of == token_of, 1.0 / PAIR_POOL, 0.0).astype(bf16)
    features = pair_w.shape[0]
    for b in range(0, n, 2):
        columns = slice(b * width, (b + 2) * width)
        pair = [
            emb[k].astype(f32) + (part[1, k].astype(f32) + other[1, k].astype(f32))
            for k in (b, b + 1)
        ]
        normed[:, columns] = jnp.concatenate(pair, axis=0).T.astype(bf16)
    pair_pool = jnp.dot(pool, normed[...], preferred_element_type=f32).astype(bf16)
    projected = jnp.dot(pair_pool, rowcol[...], preferred_element_type=f32)
    projected = projected.astype(bf16).astype(f32)
    cols[s] = projected[:, features:]
    col_copies = []
    for d in range(1, n):
        to = {"seq": (s + d) % n}
        col_copies.append(remote(cols.at[s], cols.at[s], col_sem, (d,), to))
    tokens_out[...] = normed[own_tokens, :]
    for copy in col_copies:
        copy.wait_recv()
    row_part = projected[:, None, :features]
    for j in range(n // 2):
        column = cols[c * (n // 2) + j]
        hid[:, pl.ds(j * rows_n, rows_n), :] = jax.nn.gelu(
            row_part + column[None, :, :], approximate=True
        )
    hidden = hid[...].reshape(rows_n * (n // 2) * rows_n, features).astype(bf16)
    result = jnp.dot(hidden, pair_w[...], preferred_element_type=f32)
    pair_out[...] = result.reshape(pair_out.shape).astype(bf16)
    for copy in started:
        copy.wait_send()


def on_device_fused(
    signal,
    conv_weight,
    conv_gain,
    embed_weight,
    attn_gain,
    query_weight,
    keyvalue_weight,
    output_weight,
    rowcol_weight,
    pair_weight,
):
    bf16, f32 = jnp.bfloat16, jnp.float32
    n = lax.axis_size("seq")
    nz = n // Y
    positions, half = signal.shape
    taps, channels, _ = conv_weight.shape
    count = positions // POOL
    width = embed_weight.shape[1]
    q_cols = query_weight.shape[1] // 2
    heads = q_cols // DK
    kv_cols = keyvalue_weight.shape[1]
    rows_n = count // PAIR_POOL
    features = pair_weight.shape[0]
    any_spec = pl.BlockSpec(memory_space=pl.ANY)
    vmem = pl.BlockSpec(memory_space=pltpu.VMEM)
    dma = pltpu.SemaphoreType.DMA
    tokens, pair = pl.pallas_call(
        functools.partial(fused_kernel, taps, heads),
        out_shape=(
            jax.ShapeDtypeStruct((count // 2, n * width), bf16),
            jax.ShapeDtypeStruct((rows_n, rows_n * n // 2, features), bf16),
        ),
        in_specs=[any_spec, any_spec, vmem, any_spec, vmem]
        + [any_spec, any_spec, any_spec, vmem, vmem],
        out_specs=(vmem, vmem),
        scratch_shapes=[
            pltpu.VMEM((2, half, positions), bf16),
            pltpu.VMEM((2, half, positions), bf16),
            pltpu.VMEM((2 * half, taps * count), bf16),
            pltpu.VMEM((EDGE, half), bf16),
            pltpu.VMEM((2, 2, EDGE, half), bf16),
            pltpu.VMEM((taps, half, channels), bf16),
            pltpu.VMEM((n, width, half), bf16),
            pltpu.VMEM((n, width, q_cols), bf16),
            pltpu.VMEM((n, width, kv_cols), bf16),
            pltpu.VMEM((n, width, heads * DV), bf16),
            pltpu.VMEM((2, n, width, count), bf16),
            pltpu.VMEM((2, n, width, count), bf16),
            pltpu.VMEM((n, width, count), bf16),
            pltpu.VMEM((count, n * width), bf16),
            pltpu.VMEM((n, count, kv_cols), bf16),
            pltpu.VMEM((n, rows_n, features), f32),
            pltpu.VMEM((rows_n, rows_n * n // 2, features), f32),
            dma((5 + taps,)),
            dma((2, 5)),
            dma((2, 4, 4 * nz)),
            dma((2, n)),
            dma((2, n)),
            dma((2, n)),
            dma((2, 2, n)),
            dma((2, n)),
        ],
        compiler_params=pltpu.CompilerParams(
            collective_id=0, has_side_effects=True, vmem_limit_bytes=60 * 1024 * 1024
        ),
    )(
        signal.T,
        jnp.swapaxes(conv_weight, 1, 2),
        conv_gain.reshape(2, half),
        embed_weight.T,
        attn_gain.reshape(1, n * width),
        query_weight,
        keyvalue_weight,
        output_weight.T,
        rowcol_weight,
        pair_weight,
    )
    return tokens, pair


def fits(mesh):
    n = mesh.shape["seq"]
    return n == 8 and mesh.shape["col"] == 2 and mesh.shape["grp"] == 2


def solution(mesh):
    placed = (
        P(("grp", "seq"), "col"),
        P(None, None, "col"),
        P(),
        P("col", "seq"),
        P(),
        P("seq", None),
        P("seq", None),
        P(None, "seq"),
        P(),
        P(),
    )
    return jax.shard_map(
        on_device_fused if fits(mesh) else on_device,
        mesh=mesh,
        in_specs=placed,
        out_specs=(P(("grp", "seq", "col"), None), P(("grp", "seq"), "col", None)),
        check_vma=False,
    )
```
